256 devices in a mesh: graph: 128 (over x, y, z), mp: 2 (over core).
Axes of the slice: x: 4, y: 4, z: 8, core: 2. Of those that a mesh axis runs over, the one named last changes fastest.
Arguments:
- messages: bfloat16 [131072, 512], P('graph', 'mp'), may hold values from -6 to 6
- basis_blocks: bfloat16 [12288, 128, 128], P('graph'), may hold values from -0.5 to 0.5
- source_block: int32 [12288], P('graph'), may hold values from 0 to 7
- target_owner: int32 [12288, 1], P('graph'), may hold values from 0 to 127; in each aligned block of 96 rows (0 to 95, 96 to 191, ...) at most 2 rows name the same one
- target_block: int32 [12288], P('graph'), may hold values from 0 to 7
- row_counts: int32 [12288], P('graph'), may hold values from 1 to 128
- reverse_block: int32 [1024], P('graph'), may hold values from 0 to 1023, as said below
- valid_edges: int32 [128], P('graph'), may hold values from 512 to 1024
- weight_in: bfloat16 [3, 512, 512], P(None, None, 'mp'), may hold values from -0.25 to 0.25
- weight_out: bfloat16 [3, 512, 512], P(None, 'mp'), may hold values from -0.25 to 0.25
Outputs:
- updated: bfloat16 [131072, 512], P('graph', 'mp')
The draws below stay inside these ranges and needn't reach their ends.
Inputs may be any that keep to these rules, and one draw needn't show every extreme that they name: `target_owner`: among the 96 triplet blocks of one device, no owner is named more than 2 times, a bound that some block reaches. `reverse_block`: an involution on edge blocks. Of device g's 8 blocks, the first 2 pair with blocks 2 to 3 of device (g - 1) mod 128, blocks 2 to 3 pair with the first 2 of device (g + 1) mod 128, and the others pair with blocks of device g itself.
All inputs are finite; a program needn't handle non-finite values.
Results may differ from the reference program's by a relative error of at most 0.0073.
Values may be sent and summed in bfloat16 or wider, within the bound.
A program may use at most 128 MiB of HBM per device.

```python
import math
import jax
import jax.numpy as jnp
import numpy as np
from jax import lax

H = 512
MLPS = 3
BLK = 128
E_DEV = 1024
SLOTS = 96
EB = 8
RB = 2
CAP = 2
EDGES = 131072
NBLOCKS = 1024
SLOTS_ALL = 12288
N_GRAPH = 128


def draw_reverse_block(key, part):
    key_edge, key_inner = jax.random.split(jax.random.fold_in(key, 7))
    devices = jnp.arange(N_GRAPH, dtype=jnp.int32)
    inner_count = EB - 2 * RB

    def edge_order(device):
        return jax.random.permutation(jax.random.fold_in(key_edge, device), RB).astype(jnp.int32)

    def inner_order(device):
        return jax.random.permutation(jax.random.fold_in(key_inner, device), inner_count).astype(jnp.int32)
    edge_perm = jax.vmap(edge_order)(devices)
    edge_inverse = jnp.argsort(edge_perm, axis=1).astype(jnp.int32)
    inner_perm = jax.vmap(inner_order)(devices)
    swapped = inner_perm.reshape(N_GRAPH, inner_count // 2, 2)[:, :, ::-1].reshape(N_GRAPH, inner_count)
    partner = jnp.zeros((N_GRAPH, inner_count), jnp.int32).at[devices[:, None], inner_perm].set(swapped)
    previous = (devices - 1) % N_GRAPH
    following = (devices + 1) % N_GRAPH
    head = previous[:, None] * EB + RB + edge_perm
    second = following[:, None] * EB + edge_inverse[following]
    middle = devices[:, None] * EB + 2 * RB + partner
    return jnp.concatenate([head, second, middle], axis=1).reshape(-1).astype(jnp.int32)


def plant(values, stream_key, smallest, high):
    extent = values.shape
    place = [jax.random.randint(jax.random.fold_in(stream_key, axis), (), 0, extent[axis]) for axis in range(len(extent))]
    values = values.at[tuple(place)].set(smallest)
    longest = extent.index(max(extent))
    place[longest] = (place[longest] + 1) % extent[longest]
    return values.at[tuple(place)].set(high)


def levels(stream_key, extent, cuts, smallest, largest):
    factor_of = 1.0
    for dim, blocks in cuts:
        heights = jax.random.uniform(jax.random.fold_in(jax.random.fold_in(stream_key, 6), dim), (blocks,), jnp.float32, smallest / len(cuts), largest / len(cuts))
        factor_of = factor_of * jnp.repeat(jnp.exp(heights), extent[dim] // blocks).reshape((-1,) + (1,) * (len(extent) - 1 - dim))
    return factor_of


def routed_block(own_key, own, number, rows, amount, top, most, slope):
    order = jax.random.permutation(own_key, amount)
    crowded, ordinary = shares(amount, rows * top, most, slope, True), shares(amount, rows * top, most, slope, False)
    places = jnp.arange(amount)

    def named(sizes, rotation):
        used = int((sizes > 0).sum())
        fixed = max(1, used // 4)
        shifted = fixed + (places - fixed + rotation * (used - fixed)) % max(1, amount - fixed)
        return jnp.zeros((amount,), jnp.int32).at[order[jnp.where(places < fixed, places, shifted)]].set(jnp.asarray(sizes, jnp.int32))

    sizes = jnp.where(number % 4 == 0, named(crowded, number // 4), named(ordinary, number - number // 4 - 1))
    mixed = jax.random.permutation(jax.random.fold_in(own, 3), amount)
    giver, taker = mixed[0:amount // 2 * 2:2], mixed[1:amount // 2 * 2:2]
    slack = jnp.minimum(sizes[giver] - 1, most - sizes[taker]) // 2
    slack = jnp.where((giver == order[0]) | (taker == order[0]) | (sizes[taker] == 0), 0, jnp.maximum(slack, 0))
    shifted = jax.random.randint(jax.random.fold_in(own, 4), (amount // 2,), 0, 1 << 20) % (slack + 1)
    sizes = sizes.at[giver].add(-shifted).at[taker].add(shifted)
    labels = jnp.searchsorted(jnp.cumsum(sizes), jnp.arange(rows * top), side="right").astype(jnp.int32)
    grid = labels.reshape(top, rows).T
    grid = grid[jax.random.permutation(jax.random.fold_in(own, 1), rows)]
    rotation = jax.random.randint(jax.random.fold_in(own, 2), (rows, 1), 0, top)
    return jnp.take_along_axis(grid, (jnp.arange(top)[None, :] + rotation) % top, axis=1)


def shares(count, total, reach, lean, full):
    portions = [(1 << 20) // math.isqrt(rank ** lean) + 1 for rank in range(1, count + 1)]
    largest = reach if full else min(reach, max(-(-total // count), total * portions[0] // sum(portions)))
    least = 1 if total - largest >= count - 1 else 0
    given, rest = [largest] + [least] * (count - 1), total - largest - least * (count - 1)
    while rest > 0:
        movable = [i for i in range(1, count) if given[i] < largest] or [i for i in range(1, count) if given[i] < reach]
        whole, budget = sum([portions[i] for i in movable]), rest
        for i in movable:
            extra = min(reach - given[i], max(1, budget * portions[i] // whole), rest)
            given[i] = given[i] + extra
            rest = rest - extra
    return np.array(given)


def bell_draw(key, shape, deviation, bound, cuts=(), kind=jnp.bfloat16):
    gain = levels(key, shape, cuts, -0.22, 0.18) if cuts else 1.0
    values = jax.random.normal(key, shape, jnp.float32) * deviation * gain
    return jnp.minimum(jnp.maximum(values, -bound), bound).astype(kind)


def setup_inputs(seed: int = 0) -> dict:
    splits = jax.random.split(jax.random.key(seed), 11)
    messages = bell_draw(splits[0], (EDGES, H), 1.0, 6.0, ((0, 128), (1, 2)))
    basis_blocks = bell_draw(splits[1], (SLOTS_ALL, BLK, BLK), BLK ** -0.5, 0.5, ((0, 128),))
    source_block = plant(jax.random.randint(splits[2], (SLOTS_ALL,), 0, EB), jax.random.fold_in(splits[2], 1), 0, EB - 1).astype(jnp.int32)
    target_owner_keys = jax.random.split(jax.random.fold_in(splits[3], 1), SLOTS_ALL // SLOTS)
    target_owner_turns = jax.random.permutation(jax.random.fold_in(splits[3], 3), SLOTS_ALL // SLOTS)
    target_owner = jax.vmap(lambda own, number: routed_block(jax.random.fold_in(splits[3], 2), own, number, SLOTS, N_GRAPH, 1, CAP, 2))(target_owner_keys, target_owner_turns).reshape((SLOTS_ALL, 1))
    target_block = plant(jax.random.randint(splits[4], (SLOTS_ALL,), 0, EB), jax.random.fold_in(splits[4], 1), 0, EB - 1).astype(jnp.int32)
    row_counts = plant(jax.random.randint(splits[5], (SLOTS_ALL,), 1, BLK + 1), jax.random.fold_in(splits[5], 1), 1, BLK).astype(jnp.int32)
    reverse_block = draw_reverse_block(jax.random.fold_in(splits[10], 71), 0)
    valid_edges = plant(jax.random.randint(splits[7], (N_GRAPH,), E_DEV // 2, E_DEV + 1), jax.random.fold_in(splits[7], 1), E_DEV // 2, E_DEV).astype(jnp.int32)
    weight_in = bell_draw(splits[8], (MLPS, H, H), H ** -0.5, 0.25, ((2, 2),))
    weight_out = bell_draw(splits[9], (MLPS, H, H), H ** -0.5, 0.25, ((1, 2),))
    return dict(messages=messages, basis_blocks=basis_blocks, source_block=source_block, target_owner=target_owner, target_block=target_block, row_counts=row_counts, reverse_block=reverse_block, valid_edges=valid_edges, weight_in=weight_in, weight_out=weight_out)


pair_scale = 0.7071067811865476


def reference(messages, basis_blocks, source_block, target_owner, target_block, row_counts, reverse_block, valid_edges, weight_in, weight_out):
    block_view = messages.reshape(NBLOCKS, BLK, H)
    row_index = jnp.arange(BLK, dtype=jnp.int32)

    def per_device(total, inputs):
        device, basis, source, owner, target, counts = inputs
        gathered = block_view[(device * EB + source).astype(jnp.int32)]
        product = jnp.einsum('str,src->stc', basis.astype(jnp.float32), gathered.astype(jnp.float32))
        keep = row_index[None, :] < counts[:, None]
        product = jnp.where(keep[:, :, None], product, 0.0).astype(jnp.bfloat16)
        target_global = (owner * EB + target).astype(jnp.int32)
        total = total.at[target_global].add(product.astype(jnp.float32))
        return total, None

    scanned = (jnp.arange(N_GRAPH, dtype=jnp.int32),
               basis_blocks.reshape(N_GRAPH, SLOTS, BLK, BLK),
               source_block.reshape(N_GRAPH, SLOTS),
               target_owner[:, 0].reshape(N_GRAPH, SLOTS),
               target_block.reshape(N_GRAPH, SLOTS),
               row_counts.reshape(N_GRAPH, SLOTS))
    aggregate, _ = lax.scan(per_device, jnp.zeros((NBLOCKS, BLK, H), jnp.float32), scanned)
    combined = (block_view.astype(jnp.float32) + aggregate).astype(jnp.bfloat16)
    swapped = combined[reverse_block]
    state = ((combined.astype(jnp.float32) + swapped.astype(jnp.float32)) * pair_scale).reshape(EDGES, H)
    for layer in range(MLPS):
        layer_input = state.astype(jnp.bfloat16)
        hidden = jax.nn.silu(jnp.dot(layer_input, weight_in[layer], preferred_element_type=jnp.float32)).astype(jnp.bfloat16)
        state = state + jnp.dot(hidden, weight_out[layer], preferred_element_type=jnp.float32)
    position = jnp.arange(EDGES, dtype=jnp.int32)
    keep_edge = (position % E_DEV) < valid_edges[position // E_DEV]
    return jnp.where(keep_edge[:, None], state, 0.0).astype(jnp.bfloat16)
```

```python
import functools

import jax
import jax.numpy as jnp
from jax import lax
from jax.experimental import pallas as pl
from jax.experimental.pallas import tpu as pltpu
from jax.sharding import PartitionSpec as P

BLK = 128
MLPS = 3
NX, NY, NZ = 4, 4, 8
PLANE = NX * NY
EB = 8
SLOTS = 96
SCALE = 0.7071067811865476
MESH = pl.DeviceIdType.MESH
VMEM = pltpu.VMEM
SMEM = pltpu.SMEM


def coords():
    g = lax.axis_index("graph")
    return g, g // (NY * NZ), (g // NZ) % NY, g % NZ, lax.axis_index("mp")


def slot_kernel(core_ref, owner_ref, source_ref, target_ref, count_ref, basis_ref, out_ref, meta_ref, used):
    c = core_ref[0]
    out_ref[...] = jnp.zeros_like(out_ref)

    def clear(i, _):
        used[i] = 0
        meta_ref[i // 8, 0, (i % 8) * 2] = 0
        meta_ref[i // 8, 0, (i % 8) * 2 + 1] = 0
        return 0

    lax.fori_loop(0, PLANE * NZ, clear, 0)
    row = lax.broadcasted_iota(jnp.int32, (BLK, BLK), 0)

    def place(t, _):
        o = owner_ref[t]
        k = used[o]
        used[o] = k + 1
        meta_ref[o // 8, 0, (o % 8) * 2 + k] = target_ref[t] * 8 + source_ref[t]

        @pl.when(k == c)
        def _():
            out_ref[o] = jnp.where(row < count_ref[t], basis_ref[t].astype(jnp.float32), 0.0).astype(jnp.bfloat16)

        return 0

    lax.fori_loop(0, SLOTS, place, 0)


def slot_blocks(core, owner, source, target, count, basis):
    smem = pl.BlockSpec(memory_space=SMEM)
    return pl.pallas_call(
        slot_kernel,
        out_shape=(
            jax.ShapeDtypeStruct((PLANE * NZ, BLK, BLK), jnp.bfloat16),
            jax.ShapeDtypeStruct((PLANE, 8, 128), jnp.int32),
        ),
        in_specs=[smem] * 5 + [pl.BlockSpec(memory_space=VMEM)],
        out_specs=(pl.BlockSpec(memory_space=VMEM), smem),
        scratch_shapes=[SMEM((PLANE * NZ,), jnp.int32)],
        name="slots",
    )(core, owner, source, target, count, basis)


def plane_kernel(msg, pb, meta, G, BB, MT, msg_s, msg_r, bas_s, bas_r, fwd_s, fwd_r, met_s, met_r, loc):
    g, x, y, z, c = coords()
    me = x * NY + y
    half, quarter = 512, 256

    def pos(dx, dy):
        return ((x + dx) % NX) * NY + (y + dy) % NY

    def dev(dx, dy):
        return (pos(dx, dy) * NZ + z, c)

    partner = (g, 1 - c)
    others = [(dx, dy) for dx in range(NX) for dy in range(NY) if (dx, dy) != (0, 0)]
    barrier = pltpu.get_barrier_semaphore()
    for d in others:
        pl.semaphore_signal(barrier, inc=1, device_id=dev(*d), device_id_type=MESH)
    pl.semaphore_signal(barrier, inc=1, device_id=partner, device_id_type=MESH)
    pl.semaphore_wait(barrier, len(others) + 1)

    def local_copy(src, dst, i):
        return pltpu.make_async_copy(src, dst, loc.at[i])

    own = [
        local_copy(msg, G.at[me], 0),
        local_copy(pb.at[pl.ds(me * NZ, NZ)], BB.at[c, me], 1),
        local_copy(meta.at[me], MT.at[me], 2),
    ]
    for cp in own:
        cp.start()

    def remote(src, dst, s, r, i, device):
        return pltpu.make_async_remote_copy(
            src_ref=src, dst_ref=dst, send_sem=s.at[i], recv_sem=r.at[i], device_id=device, device_id_type=MESH
        )

    def ab(h, a, b):
        return (a, b) if h == 0 else (b, a)

    def piece(h, a, b, part):
        p = pos(*ab(h, a, b))
        rows = {None: (h * half, half), 0: (h * half, quarter), 1: (h * half + quarter, quarter)}[part]
        return p, pl.ds(rows[0], rows[1])

    def gref(h, a, b, part):
        p, rows = piece(h, a, b, part)
        return G.at[p, rows]

    roles = {}
    sems = {}
    for h in (0, 1):
        for name in ["a1+", "a1-", "a2+", "a2-"] + [n + str(a) for n in ("b1+", "b1-", "b2+", "b2-") for a in (0, 1, 2, 3)]:
            sems[h, name] = len(sems)

    def message(h, name, sending):
        sign = 1 if name[2] == "+" else -1
        if name[:2] == "a1":
            a, b, part, step = 0, 0, None, (sign, 0)
        elif name[:2] == "a2":
            a, b, part, step = -sign, 0, (0 if sign > 0 else 1), (sign, 0)
        elif name[:2] == "b1":
            a, b, part, step = int(name[3]), 0, None, (0, sign)
        else:
            a, b, part, step = int(name[3]), -sign, (0 if sign > 0 else 1), (0, sign)
        if a % 4 == 0 and b == 0:
            src = msg.at[piece(h, 0, 0, part)[1]]
        else:
            src = gref(h, a, b, part)
        if not sending:
            src = gref(h, a - step[0], b - step[1], part)
            return remote(src, src, msg_s, msg_r, sems[h, name], dev(*ab(h, *step)))
        return remote(src, gref(h, a, b, part), msg_s, msg_r, sems[h, name], dev(*ab(h, *step)))

    started = []

    def send(h, name):
        cp = message(h, name, True)
        cp.start()
        started.append(cp)

    def recv(h, name):
        message(h, name, False).wait_recv()

    def basis_send(i):
        d = others[i]
        p = pos(*d)
        cp = remote(pb.at[pl.ds(p * NZ, NZ)], BB.at[c, me], bas_s, bas_r, i, dev(*d))
        cp.start()
        started.append(cp)

    def basis_forward(i):
        d = others[i]
        p = pos(-d[0], -d[1])
        there = BB.at[c, p]
        remote(there, there, bas_s, bas_r, i, dev(*d)).wait_recv()
        cp = remote(there, there, fwd_s, fwd_r, i, partner)
        cp.start()
        started.append(cp)

    for h in (0, 1):
        send(h, "a1+")
        send(h, "a1-")
    for h in (0, 1):
        send(h, "b1+0")
        send(h, "b1-0")
    for i, d in enumerate(others):
        cp = remote(meta.at[pos(*d)], MT.at[me], met_s, met_r, i, dev(*d))
        cp.start()
        started.append(cp)
    cp = remote(pb.at[pl.ds(me * NZ, NZ)], BB.at[c, me], fwd_s, fwd_r, len(others), partner)
    cp.start()
    started.append(cp)
    order = sorted(range(len(others)), key=lambda i: sum(min(v, 4 - v) for v in others[i]))
    for i in order[:5]:
        basis_send(i)
    for h in (0, 1):
        recv(h, "a1+")
        send(h, "a2+")
        send(h, "b1+3")
        send(h, "b1-3")
        recv(h, "a1-")
        send(h, "a2-")
        send(h, "b1+1")
        send(h, "b1-1")
    for i in order[5:10]:
        basis_send(i)
    for h in (0, 1):
        recv(h, "b1+0")
        send(h, "b2+0")
        recv(h, "b1-0")
        send(h, "b2-0")
    for h in (0, 1):
        recv(h, "a2+")
        recv(h, "a2-")
        send(h, "b1+2")
        send(h, "b1-2")
    for i in order[10:]:
        basis_send(i)
    for a in ("3", "1"):
        for h in (0, 1):
            recv(h, "b1+" + a)
            send(h, "b2+" + a)
            recv(h, "b1-" + a)
            send(h, "b2-" + a)
    for i in order[:5]:
        basis_forward(i)
    for h in (0, 1):
        recv(h, "b1+2")
        send(h, "b2+2")
        recv(h, "b1-2")
        send(h, "b2-2")
    for i in order[5:]:
        basis_forward(i)
    for a in ("0", "3", "1", "2"):
        for h in (0, 1):
            recv(h, "b2+" + a)
            recv(h, "b2-" + a)
    for i, d in enumerate(others):
        there = BB.at[1 - c, pos(-d[0], -d[1])]
        remote(there, there, fwd_s, fwd_r, i, partner).wait_recv()
        slot = MT.at[pos(-d[0], -d[1])]
        remote(slot, slot, met_s, met_r, i, dev(*d)).wait_recv()
    there = BB.at[1 - c, me]
    remote(there, there, fwd_s, fwd_r, len(others), partner).wait_recv()
    for cp in own:
        cp.wait()
    for cp in started:
        cp.wait_send()


def plane_exchange(messages, basis, meta):
    n = PLANE - 1
    any_ = pl.BlockSpec(memory_space=pl.ANY)
    dma = pltpu.SemaphoreType.DMA
    return pl.pallas_call(
        plane_kernel,
        out_shape=(
            jax.ShapeDtypeStruct((PLANE,) + messages.shape, jnp.bfloat16),
            jax.ShapeDtypeStruct((2, PLANE, NZ, BLK, BLK), jnp.bfloat16),
            jax.ShapeDtypeStruct((PLANE, 8, 128), jnp.int32),
        ),
        in_specs=[pl.BlockSpec(memory_space=VMEM)] * 2 + [any_],
        out_specs=(any_,) * 3,
        scratch_shapes=[
            dma((40,)), dma((40,)), dma((n,)), dma((n,)), dma((n + 1,)), dma((n + 1,)), dma((n,)), dma((n,)), dma((3,)),
        ],
        compiler_params=pltpu.CompilerParams(collective_id=0, has_side_effects=True),
        name="plane",
    )(messages, basis, meta)


def product_kernel(meta, g_ref, b_ref, out_ref, acc):
    p = pl.program_id(0)

    @pl.when(p == 0)
    def _():
        acc[...] = jnp.zeros_like(acc)

    def owner(zo, _):
        for k in (0, 1):
            m = meta[p, 0, zo * 2 + k]
            prod = jnp.dot(b_ref[k, 0, zo], g_ref[0, m % 8], preferred_element_type=jnp.float32)
            t = zo * EB + m // 8
            acc[t] = acc[t] + prod
        return 0

    lax.fori_loop(0, NZ, owner, 0)

    @pl.when(p == PLANE - 1)
    def _():
        def put(t, _):
            out_ref[t] = acc[t].astype(jnp.bfloat16)
            return 0

        lax.fori_loop(0, NZ * EB, put, 0)


def plane_products(meta, gathered, basis):
    width = gathered.shape[-1]
    return pl.pallas_call(
        product_kernel,
        out_shape=jax.ShapeDtypeStruct((NZ * EB, BLK, width), jnp.bfloat16),
        grid=(PLANE,),
        in_specs=[
            pl.BlockSpec(memory_space=SMEM),
            pl.BlockSpec((1, EB, BLK, width), lambda p: (p, 0, 0, 0)),
            pl.BlockSpec((2, 1, NZ, BLK, BLK), lambda p: (0, p, 0, 0, 0)),
        ],
        out_specs=pl.BlockSpec((NZ * EB, BLK, width), lambda p: (0, 0, 0)),
        scratch_shapes=[VMEM((NZ * EB, BLK, width), jnp.float32)],
        name="products",
    )(meta, gathered.reshape(PLANE, EB, BLK, width), basis)


def tail_kernel(
    rev, valid, part, msg, w_in, w_out, out,
    up_s, dn_s, up_r, dn_r, full, st, give, win2, wout2, hid, res, fin,
    z_s, z_r, rim_s, rim_r, mp_s, mp_r,
):
    g, x, y, z, c = coords()
    base = g - z
    up_dev = (base + (z + 1) % NZ, c)
    dn_dev = (base + (z + NZ - 1) % NZ, c)
    count = NX * NY * NZ
    before, after = (g + count - 1) % count, (g + 1) % count
    partner = (g, 1 - c)
    barrier = pltpu.get_barrier_semaphore()
    for d in (up_dev, dn_dev, (before, c), (after, c), partner):
        pl.semaphore_signal(barrier, inc=1, device_id=d, device_id_type=MESH)
    pl.semaphore_wait(barrier, 5)

    def remote(src, dst, s, r, i, device):
        return pltpu.make_async_remote_copy(
            src_ref=src, dst_ref=dst, send_sem=s.at[i], recv_sem=r.at[i], device_id=device, device_id_type=MESH
        )

    started = []

    def go(*args):
        cp = remote(*args)
        cp.start()
        started.append(cp)

    def chain(up, s, q):
        return (0 if up else 8) + s * 2 + q

    def blocks(q):
        return pl.ds(q * 4, 4)

    def part_of(up, s, q):
        zo = (z + 4 - s) % NZ if up else (z + 4 + s) % NZ
        return zo * EB + q * 4

    first = {True: 0, False: 1}
    recv_buf = {True: up_r, False: dn_r}
    send_buf = {True: up_s, False: dn_s}
    dest = {True: up_dev, False: dn_dev}

    def z_send(up, s, q, src):
        go(src, recv_buf[up].at[s, blocks(q)], z_s, z_r, chain(up, s, q), dest[up])

    def z_wait(up, s, q):
        there = recv_buf[up].at[s, blocks(q)]
        remote(there, there, z_s, z_r, chain(up, s, q), dest[up]).wait_recv()

    for up in (True, False):
        z_send(up, 0, first[up], part.at[pl.ds(part_of(up, 0, first[up]), 4)])
    for up in (True, False):
        q = 1 - first[up]
        z_send(up, 1, q, part.at[pl.ds(part_of(up, 1, q), 4)])
    go(w_in, win2, mp_s, mp_r, 0, partner)
    go(w_out, wout2, mp_s, mp_r, 1, partner)
    for s in (1, 2, 3):
        for q0 in (0, 1):
            for up in (True, False):
                q = first[up] if q0 == 0 else 1 - first[up]
                if s == 1 and q != first[up]:
                    continue
                z_wait(up, s - 1, q)

                def add(i, _, up=up, s=s, q=q):
                    b = q * 4 + i
                    send_buf[up][s, b] = (
                        part[part_of(up, s, q) + i].astype(jnp.float32) + recv_buf[up][s - 1, b].astype(jnp.float32)
                    ).astype(jnp.bfloat16)
                    return 0

                lax.fori_loop(0, 4, add, 0)
                z_send(up, s, q, send_buf[up].at[s, blocks(q)])
    for q in (0, 1):
        z_wait(True, 3, q)
        z_wait(False, 3, q)

        def finish(i, _, q=q):
            b = q * 4 + i
            total = part[z * EB + b].astype(jnp.float32) + up_r[3, b].astype(jnp.float32) + dn_r[3, b].astype(jnp.float32)
            full[2 + b] = (msg[b].astype(jnp.float32) + total).astype(jnp.bfloat16)
            return 0

        lax.fori_loop(0, 4, finish, 0)
        if q == 0:
            go(full.at[pl.ds(2, 2)], full.at[pl.ds(10, 2)], rim_s, rim_r, 0, (before, c))
            go(full.at[pl.ds(4, 2)], full.at[pl.ds(0, 2)], rim_s, rim_r, 1, (after, c))
    remote(full.at[pl.ds(10, 2)], full.at[pl.ds(10, 2)], rim_s, rim_r, 0, (before, c)).wait_recv()
    remote(full.at[pl.ds(0, 2)], full.at[pl.ds(0, 2)], rim_s, rim_r, 1, (after, c)).wait_recv()

    def state_of(b):
        r = rev[b]
        holder, within = r // EB, r % EB
        at = jnp.where(holder == g, 2 + within, jnp.where(holder == before, within - 2, 10 + within))
        at = jnp.clip(at, 0, EB + 3)
        return (full[2 + b].astype(jnp.float32) + full[at].astype(jnp.float32)) * SCALE

    def theirs(i, _):
        give[i] = state_of((1 - c) * 4 + i)
        return 0

    lax.fori_loop(0, 4, theirs, 0)
    go(give, st.at[c], mp_s, mp_r, 2, partner)

    def mine(i, _):
        st[c, i] = state_of(c * 4 + i)
        return 0

    lax.fori_loop(0, 4, mine, 0)
    remote(win2, win2, mp_s, mp_r, 0, partner).wait_recv()
    remote(wout2, wout2, mp_s, mp_r, 1, partner).wait_recv()
    remote(st.at[1 - c], st.at[1 - c], mp_s, mp_r, 2, partner).wait_recv()

    def silu(v):
        h = v * 0.5
        return h + h * jnp.tanh(h)

    def mm(a, b):
        return jnp.dot(a, b, preferred_element_type=jnp.float32)

    def layer(k, _):
        xin = jnp.concatenate([st[n].reshape(512, 256).astype(jnp.bfloat16) for n in (0, 1)], axis=1)
        hid[0] = silu(mm(xin, w_in[k])).astype(jnp.bfloat16)
        hid[1] = silu(mm(xin, win2[k])).astype(jnp.bfloat16)
        for n in (0, 1):
            cols = pl.ds(n * 256, 256)
            step = mm(hid[0], w_out[k, :, cols]) + mm(hid[1], wout2[k, :, cols])
            st[n] = st[n] + step.reshape(4, BLK, 256)
        return 0

    lax.fori_loop(0, MLPS, layer, 0)
    row = lax.broadcasted_iota(jnp.int32, (512, 256), 0) + c * 512
    for n in (0, 1):
        res[n] = jnp.where(row < valid[0], st[n].reshape(512, 256), 0.0).astype(jnp.bfloat16)
    go(res.at[1 - c], fin, mp_s, mp_r, 3, partner)
    out[pl.ds(c * 512, 512)] = res[c]
    remote(fin, fin, mp_s, mp_r, 3, partner).wait_recv()
    out[pl.ds((1 - c) * 512, 512)] = fin[...]
    for cp in started:
        cp.wait_send()


def tail(rev, valid, part, messages, w_in, w_out):
    rows, width = messages.shape
    vm = pl.BlockSpec(memory_space=VMEM)
    smem = pl.BlockSpec(memory_space=SMEM)
    dma = pltpu.SemaphoreType.DMA
    bf, f32 = jnp.bfloat16, jnp.float32
    chunk = (4, EB, BLK, width)
    return pl.pallas_call(
        tail_kernel,
        out_shape=jax.ShapeDtypeStruct((rows, width), bf),
        in_specs=[smem, smem, vm, vm, vm, vm],
        out_specs=vm,
        scratch_shapes=[
            VMEM(chunk, bf), VMEM(chunk, bf), VMEM(chunk, bf), VMEM(chunk, bf),
            VMEM((EB + 4, BLK, width), bf),
            VMEM((2, 4, BLK, width), f32),
            VMEM((4, BLK, width), f32),
            VMEM(w_in.shape, bf), VMEM(w_out.shape, bf),
            VMEM((2, rows // 2, width), bf),
            VMEM((2, rows // 2, width), bf),
            VMEM((rows // 2, width), bf),
            dma((16,)), dma((16,)), dma((2,)), dma((2,)), dma((4,)), dma((4,)),
        ],
        compiler_params=pltpu.CompilerParams(collective_id=1, has_side_effects=True),
        name="tail",
    )(rev, valid, part, messages.reshape(EB, BLK, width), w_in, w_out)


def local(
    messages, basis_blocks, source_block, target_owner, target_block,
    row_counts, reverse_block, valid_edges, weight_in, weight_out,
):
    core = lax.axis_index("mp").reshape(1)
    slots, meta = slot_blocks(core, target_owner[:, 0], source_block, target_block, row_counts, basis_blocks)
    gathered, basis, metas = plane_exchange(messages, slots, meta)
    part = plane_products(metas, gathered, basis)
    return tail(reverse_block, valid_edges, part, messages, weight_in, weight_out)


def solution(mesh):
    in_specs = (
        P("graph", "mp"),
        P("graph", None, None),
        P("graph"),
        P("graph", None),
        P("graph"),
        P("graph"),
        P("graph"),
        P("graph"),
        P(None, None, "mp"),
        P(None, "mp", None),
    )
    return jax.shard_map(local, mesh=mesh, in_specs=in_specs, out_specs=P("graph", "mp"), check_vma=False)
```
